32 devices in a mesh: seq: 8 (over z, x), tp: 4 (over y, core).
Axes of the slice: x: 2, y: 2, z: 4, core: 2. Of those that a mesh axis runs over, the one named last changes fastest.
Arguments:
- queries: bfloat16 [4096, 4096], P('seq', 'tp'), may hold values from -6 to 6
- keys: bfloat16 [4096, 4096], P('seq', 'tp'), may hold values from -6 to 6
- values: bfloat16 [4096, 4096], P('seq', 'tp'), may hold values from -6 to 6
- grad_out: bfloat16 [4096, 4096], P('seq', 'tp'), may hold values from -16 to 16
- out_weight: bfloat16 [4096, 4096], P('tp'), may hold values from -0.09375 to 0.09375
- norm_gain: float32 [4096], P('tp'), may hold values from 0.1 to 1.9
- doc_ids: int32 [4096], P('seq'), may hold values from 0 to 3, never falling along the last dimension, each value on 1 to 2048 neighbouring positions
Outputs:
- query_grad: bfloat16 [4096, 4096], P('seq', 'tp')
- key_grad: bfloat16 [4096, 4096], P('seq', 'tp')
- value_grad: bfloat16 [4096, 4096], P('seq', 'tp')
- out_proj_grad: float32 [4096, 4096], P('seq', 'tp')
The draws below stay inside these ranges and needn't reach their ends.
Inputs may be any that keep to these rules, and one draw needn't show every extreme that they name: `doc_ids`: document ids never fall along the sequence; each document has 1 to 2048 positions and one has exactly 2048.
All inputs are finite; a program needn't handle non-finite values.
Results may differ from the reference program's by a relative error of at most 0.012.
Values may be sent and summed in bfloat16 or wider, within the bound.
A program may use at most 128 MiB of HBM per device.

```python
import math
import jax
import jax.numpy as jnp
import numpy as np
from jax import lax

D = 4096
HEADS = 32
HEAD_DIM = 128
DOCS = 4
BLOCK = 512
TOKENS = 4096


def spiked(values, own_key, source, target, shards_of, factor):
    def block_of(axis_at):
        return (jnp.arange(values.shape[axis_at]) // (values.shape[axis_at] // shards_of)).reshape((-1,) + (1,) * (values.ndim - 1 - axis_at))

    near = jax.random.permutation(own_key, shards_of)[block_of(target)]
    second = (block_of(target) + shards_of // 2) % shards_of
    return jnp.where((block_of(source) == near) | (block_of(source) == second), factor * values, values)


def block_scale(own_key, extent, pieces, low, largest):
    level, own = 1.0, jax.random.fold_in(own_key, 6)
    for axis_at, parts in pieces:
        draws = jnp.exp(jax.random.uniform(jax.random.fold_in(own, axis_at), (parts,), jnp.float32, low / len(pieces), largest / len(pieces)))
        level = level * jnp.repeat(draws, extent[axis_at] // parts).reshape([-1 if axis == axis_at else 1 for axis in range(len(extent))])
    return level


def profile(number_of, total, bound, skew):
    portions = [(1 << 20) // math.isqrt(rank ** skew) + 1 for rank in range(2, number_of + 1)]
    rest, counts = total - bound - (number_of - 1), [1] * (number_of - 1)
    while rest > 0:
        free = [i for i in range(number_of - 1) if counts[i] < bound]
        pool, budget = sum([portions[i] for i in free]), rest
        for i in free:
            more = min(bound - counts[i], max(1, budget * portions[i] // pool), rest)
            counts[i] = counts[i] + more
            rest = rest - more
    return np.array([bound] + counts)


def uneven(rng, count, total, most, skew):
    if count == 2:
        one = jax.random.randint(rng, (), max(1, total - most), min(most, total - 1) + 1)
        return jnp.stack([one, total - one])
    lengths = jnp.asarray(profile(count, total, most, skew), jnp.int32)
    pairs = (count - 1) // 2
    donor, sink = lengths[1:1 + 2 * pairs:2], lengths[2:2 + 2 * pairs:2]
    margin = jnp.minimum(donor - 1, most - sink)
    shifted = jax.random.randint(jax.random.fold_in(rng, 1), (pairs,), 0, 1 << 20) % (margin + 1)
    lengths = lengths.at[1:1 + 2 * pairs:2].set(donor - shifted).at[2:2 + 2 * pairs:2].set(sink + shifted)
    return lengths[jax.random.permutation(jax.random.fold_in(rng, 2), count)]


def centred(rng, dims, scale, most, cuts=(), held_as=jnp.bfloat16):
    loudness = block_scale(rng, dims, cuts, -0.22, 0.18) if cuts else 1.0
    result = jax.random.normal(rng, dims, jnp.float32) * scale * loudness
    return jnp.minimum(jnp.maximum(result, -most), most).astype(held_as)


def gaussian_with(key, dims, deviation, most, shards, heavy, dtype=jnp.bfloat16):
    entries = deviation * jax.random.normal(key, dims, jnp.float32)
    if shards:
        entries = entries * block_scale(key, dims, shards, -0.22, 0.18)
    return jnp.clip(spiked(entries, jax.random.fold_in(key, 3), *heavy), -most, most).astype(dtype)


def setup_inputs(seed: int = 0) -> dict:
    splits = jax.random.split(jax.random.key(seed), 8)
    queries = centred(splits[0], (TOKENS, HEADS * HEAD_DIM), 1.0, 6.0, ((0, 8), (1, 4)))
    keys = centred(splits[1], (TOKENS, HEADS * HEAD_DIM), 1.0, 6.0, ((0, 8), (1, 4)))
    values = centred(splits[2], (TOKENS, HEADS * HEAD_DIM), 1.0, 6.0, ((0, 8), (1, 4)))
    grad_out = gaussian_with(splits[3], (TOKENS, D), 4.0, 16.0, ((0, 8), (1, 4)), (0, 1, 8, 2.0))
    out_weight = centred(splits[4], (HEADS * HEAD_DIM, D), (HEADS * HEAD_DIM) ** -0.5, 0.09375, ((0, 4),))
    norm_gain = jnp.clip(1.0 + 0.18 * jax.random.normal(splits[5], (HEADS * HEAD_DIM,), jnp.float32), 0.1, 1.9)
    doc_ids = jnp.searchsorted(jnp.cumsum(uneven(splits[6], DOCS, TOKENS, TOKENS // 2, 2)), jnp.arange(TOKENS), side="right").astype(jnp.int32)
    return {"queries": queries, "keys": keys, "values": values, "grad_out": grad_out, "out_weight": out_weight, "norm_gain": norm_gain, "doc_ids": doc_ids}


EPS = 1e-06

def feature(x):
    return jnp.where(x > 0, x + 1.0, jnp.exp(jnp.minimum(x, 0.0)))

def feature_slope(x):
    return jnp.where(x > 0, 1.0, jnp.exp(jnp.minimum(x, 0.0)))

def combine(earlier, later):
    state_early, tag_early = earlier
    state_late, tag_late = later
    vacant = tag_late < 0
    joined = state_late + jnp.where(tag_early == tag_late, state_early, 0.0)
    return (jnp.where(vacant, state_early, joined), jnp.where(vacant, tag_early, tag_late))

def reference(queries, keys, values, grad_out, out_weight, norm_gain, doc_ids):
    block_count = TOKENS // BLOCK
    feat_q = feature(queries.astype(jnp.float32)).astype(jnp.bfloat16)
    feat_k = feature(keys.astype(jnp.float32)).astype(jnp.bfloat16)

    def split(array):
        return array.reshape(block_count, BLOCK, HEADS, HEAD_DIM)
    doc_float = doc_ids.astype(jnp.float32).reshape(block_count, BLOCK)
    positions = jnp.arange(BLOCK)
    causal = positions[:, None] >= positions[None, :]
    gain = norm_gain.astype(jnp.float32).reshape(HEADS, HEAD_DIM)

    def pair_weights(query_block, key_block, doc_block):
        allowed = causal & (doc_block[:, None] == doc_block[None, :])
        scores = jnp.einsum('thd,shd->hts', query_block.astype(jnp.float32), key_block.astype(jnp.float32))
        return (jnp.where(allowed[None], scores, 0.0).astype(jnp.bfloat16), allowed)
    start_state = (jnp.zeros((HEADS, HEAD_DIM, HEAD_DIM), jnp.float32), jnp.array(-1.0, jnp.float32))

    def forward_step(carry, items):
        query_block, key_block, value_block, doc_block = items
        state, tag = carry
        weight, allowed = pair_weights(query_block, key_block, doc_block)
        inner = jnp.einsum('hts,she->the', weight.astype(jnp.float32), value_block.astype(jnp.float32))
        rounded = state.astype(jnp.bfloat16).astype(jnp.float32)
        outer = jnp.einsum('thd,hde->the', query_block.astype(jnp.float32), rounded)
        attn = inner + jnp.where((doc_block == tag)[:, None, None], outer, 0.0)
        last_doc = doc_block[-1]
        chosen = (doc_block == last_doc)[:, None, None]
        summary = jnp.einsum('shd,she->hde', jnp.where(chosen, key_block.astype(jnp.float32), 0.0), value_block.astype(jnp.float32))
        return (combine(carry, (summary, last_doc)), (attn, state, tag))
    _, (attn, states, tags) = lax.scan(forward_step, start_state, (split(feat_q), split(feat_k), split(values), doc_float))
    inv_rms = lax.rsqrt(lax.optimization_barrier(jnp.mean(attn * attn, axis=-1, keepdims=True)) + EPS)
    normed = (attn * inv_rms * gain).astype(jnp.bfloat16)
    upstream = jnp.dot(grad_out, out_weight.T, preferred_element_type=jnp.float32)
    scaled = split(upstream) * gain
    grad_attn = (scaled * inv_rms - attn * inv_rms ** 3 * lax.optimization_barrier(jnp.mean(attn * scaled, axis=-1, keepdims=True))).astype(jnp.bfloat16)
    out_proj_grad = jnp.dot(grad_out.T, normed.reshape(TOKENS, HEADS * HEAD_DIM), preferred_element_type=jnp.float32) * (1.0 / math.sqrt(TOKENS))

    def backward_step(carry, items):
        query_block, key_block, value_block, doc_block, grad_block, state, tag, raw_query, raw_key = items
        dstate, dtag = carry
        weight, allowed = pair_weights(query_block, key_block, doc_block)
        qf = query_block.astype(jnp.float32)
        kf = key_block.astype(jnp.float32)
        vf = value_block.astype(jnp.float32)
        gf = grad_block.astype(jnp.float32)
        grad_weight = jnp.where(allowed[None], jnp.einsum('the,she->hts', gf, vf), 0.0).astype(jnp.bfloat16)
        dround = dstate.astype(jnp.bfloat16).astype(jnp.float32)
        sround = state.astype(jnp.bfloat16).astype(jnp.float32)
        later_rows = (doc_block == dtag)[:, None, None]
        earlier_rows = (doc_block == tag)[:, None, None]
        value_part = jnp.einsum('hts,the->she', weight.astype(jnp.float32), gf) + jnp.where(later_rows, jnp.einsum('shd,hde->she', kf, dround), 0.0)
        key_part = jnp.einsum('hts,thd->shd', grad_weight.astype(jnp.float32), qf) + jnp.where(later_rows, jnp.einsum('she,hde->shd', vf, dround), 0.0)
        query_part = jnp.einsum('hts,shd->thd', grad_weight.astype(jnp.float32), kf) + jnp.where(earlier_rows, jnp.einsum('the,hde->thd', gf, sround), 0.0)
        query_out = (query_part * feature_slope(raw_query.astype(jnp.float32))).astype(jnp.bfloat16)
        key_out = (key_part * feature_slope(raw_key.astype(jnp.float32))).astype(jnp.bfloat16)
        first_doc = doc_block[0]
        chosen = (doc_block == first_doc)[:, None, None]
        summary = jnp.einsum('thd,the->hde', jnp.where(chosen, qf, 0.0), gf)
        return (combine(carry, (summary, first_doc)), (query_out, key_out, value_part.astype(jnp.bfloat16)))
    items = (split(feat_q), split(feat_k), split(values), doc_float, grad_attn, states, tags, split(queries), split(keys))
    _, (query_grad, key_grad, value_grad) = lax.scan(backward_step, start_state, items, reverse=True)
    shape = (TOKENS, HEADS * HEAD_DIM)
    return (query_grad.reshape(shape), key_grad.reshape(shape), value_grad.reshape(shape), out_proj_grad)
```

```python
import math

import jax
import jax.numpy as jnp
from jax import lax
from jax.experimental import pallas as pl
from jax.experimental.pallas import tpu as pltpu
from jax.sharding import PartitionSpec as P

HEAD = 128
EPS = 1e-06
PAD = 16
BF = jnp.bfloat16
F32 = jnp.float32


def feature(x):
    return jnp.where(x > 0, x + 1.0, jnp.exp(jnp.minimum(x, 0.0)))


def slope(x):
    return jnp.where(x > 0, 1.0, jnp.exp(jnp.minimum(x, 0.0)))


def dot(a, b, ca, cb):
    return lax.dot_general(a, b, (((ca,), (cb,)), ((), ())), preferred_element_type=F32)


def causal_mask(col, row):
    rows = col.shape[0]
    at = lax.broadcasted_iota(jnp.int32, (rows, rows), 0)
    to = lax.broadcasted_iota(jnp.int32, (rows, rows), 1)
    return (at >= to) & (col == row)


def summary_kernel(k_ref, v_ref, col_ref, o_ref):
    h = pl.program_id(0)
    rows = k_ref.shape[0]
    col = col_ref[...]
    last = col[rows - 1 : rows, :]
    picked = jnp.where(col == last, feature(k_ref[...].astype(F32)), 0.0).astype(BF)
    o_ref[pl.ds(pl.multiple_of(h * HEAD, HEAD), HEAD), :] = dot(picked, v_ref[...], 0, 0).astype(BF)
    tail = o_ref.shape[0] - PAD
    o_ref[tail:, :] = jnp.broadcast_to(last, (PAD, HEAD)).astype(BF)


def attn_kernel(q_ref, k_ref, v_ref, s_ref, col_ref, row_ref, gain_ref, attn_ref, normed_ref):
    col = col_ref[...]
    fq = feature(q_ref[...].astype(F32)).astype(BF)
    fk = feature(k_ref[...].astype(F32)).astype(BF)
    weight = jnp.where(causal_mask(col, row_ref[...]), dot(fq, fk, 1, 1), 0.0).astype(BF)
    attn = dot(weight, v_ref[...], 1, 0)
    attn = attn + jnp.where(col == col[0:1, :], dot(fq, s_ref[...], 1, 0), 0.0)
    inv = lax.rsqrt(jnp.mean(attn * attn, axis=-1, keepdims=True) + EPS)
    attn_ref[...] = attn
    normed_ref[...] = (attn * inv * gain_ref[...]).astype(BF)


def upstream_kernel(order_ref, g_ref, w_ref, q_ref, attn_ref, col_ref, gain_ref, o_ref, sum_ref):
    i = pl.program_id(0)
    pieces, _, width = g_ref.shape
    cols = w_ref.shape[0]
    total = None
    for p in range(pieces):
        start = pl.multiple_of(order_ref[p] * width, width)
        term = dot(g_ref[p], w_ref[:, pl.ds(start, width)], 1, 1)
        total = term if total is None else total + term
    col = col_ref[...]
    first = col[0:1, :]
    for h in range(cols // HEAD):
        at = slice(h * HEAD, (h + 1) * HEAD)
        attn = attn_ref[:, at]
        inv = lax.rsqrt(jnp.mean(attn * attn, axis=-1, keepdims=True) + EPS)
        scaled = total[:, at] * gain_ref[:, at]
        mean = jnp.mean(attn * scaled, axis=-1, keepdims=True)
        grad = (scaled * inv - attn * (inv * inv * inv) * mean).astype(BF)
        o_ref[:, at] = grad
        picked = jnp.where(col == first, feature(q_ref[:, at].astype(F32)), 0.0).astype(BF)
        to = pl.multiple_of(i * cols + h * HEAD, HEAD)
        sum_ref[pl.ds(to, HEAD), :] = dot(picked, grad, 0, 0).astype(BF)
    tail = sum_ref.shape[0] - PAD
    sum_ref[tail:, :] = jnp.broadcast_to(first, (PAD, HEAD)).astype(BF)


def grads_kernel(
    q_ref, k_ref, v_ref, g_ref, s_ref, d_ref, col_ref, row_ref, oq_ref, ok_ref, ov_ref
):
    col = col_ref[...]
    rows = col.shape[0]
    mask = causal_mask(col, row_ref[...])
    q = q_ref[...].astype(F32)
    k = k_ref[...].astype(F32)
    v = v_ref[...]
    g = g_ref[...]
    fq = feature(q).astype(BF)
    fk = feature(k).astype(BF)
    weight = jnp.where(mask, dot(fq, fk, 1, 1), 0.0).astype(BF)
    gw = jnp.where(mask, dot(g, v, 1, 1), 0.0).astype(BF)
    early = col == col[0:1, :]
    late = col == col[rows - 1 : rows, :]
    s = s_ref[...]
    d = d_ref[...]
    vp = dot(weight, g, 0, 0) + jnp.where(late, dot(fk, d, 1, 0), 0.0)
    ov_ref[...] = vp.astype(BF)
    kp = dot(gw, fq, 0, 0) + jnp.where(late, dot(v, d, 1, 1), 0.0)
    ok_ref[...] = (kp * slope(k)).astype(BF)
    qp = dot(gw, fk, 1, 0) + jnp.where(early, dot(g, s, 1, 1), 0.0)
    oq_ref[...] = (qp * slope(q)).astype(BF)


def join(early, late):
    same = early[-1:, :1] == late[-1:, :1]
    body = late[:-PAD].astype(F32) + jnp.where(same, early[:-PAD].astype(F32), 0.0)
    return jnp.concatenate([body.astype(BF), late[-PAD:]], axis=0)


def local(queries, keys, values, grad_out, out_weight, norm_gain, doc_ids):
    rows, feats = queries.shape
    heads = feats // HEAD
    n = lax.axis_size("seq")
    tp = lax.axis_size("tp")
    xs = 2
    depth = n // xs
    me = lax.axis_index("seq")
    x = me % xs
    z = me // xs
    j = lax.axis_index("tp")
    model = out_weight.shape[1]
    width = model // tp
    mrows = model // n
    factor = 1.0 / math.sqrt(rows * n)
    docs = doc_ids.astype(F32)
    col = docs[:, None]
    row = docs[None, :]
    gain = norm_gain[None, :]

    swap_x = [(i, i ^ 1) for i in range(n)]

    def shift(value, step):
        pairs = [(i, i + step * xs) for i in range(n) if 0 <= i + step * xs < n]
        return lax.ppermute(value, "seq", pairs)

    def gather_tp(value):
        pieces = [value]
        bits = tp.bit_length() - 1
        for b in reversed(range(bits)):
            pairs = [(i, i ^ (1 << b)) for i in range(tp)]
            got = [lax.ppermute(piece, "tp", pairs) for piece in pieces]
            pieces = pieces + got
        offsets = [0]
        for b in reversed(range(bits)):
            offsets = offsets + [o ^ (1 << b) for o in offsets]
        ranked = sorted(range(tp), key=lambda r: offsets[r])
        return [pieces[r] for r in ranked]

    head_spec = pl.BlockSpec((rows, HEAD), lambda h: (0, h))
    state_spec = pl.BlockSpec((HEAD, HEAD), lambda h: (h, 0))
    col_spec = pl.BlockSpec((rows, 1), lambda h: (0, 0))
    row_spec = pl.BlockSpec((1, rows), lambda h: (0, 0))
    gain_spec = pl.BlockSpec((1, HEAD), lambda h: (0, h))
    sum_shape = jax.ShapeDtypeStruct((feats + PAD, HEAD), BF)
    sum_spec = pl.BlockSpec((feats + PAD, HEAD), lambda h: (0, 0))
    wide = jax.ShapeDtypeStruct((rows, feats), BF)

    def cost(flops, size):
        return pl.CostEstimate(flops=flops, bytes_accessed=size, transcendentals=0)

    sent = lax.dynamic_slice(grad_out, (0, (1 - x) * mrows), (rows, mrows))
    theirs = lax.ppermute(sent, "seq", swap_x)
    whole = gather_tp(grad_out)
    summary = pl.pallas_call(
        summary_kernel,
        grid=(heads,),
        in_specs=[head_spec, head_spec, col_spec],
        out_specs=sum_spec,
        out_shape=sum_shape,
        cost_estimate=cost(2 * rows * HEAD * feats, 4 * rows * feats),
        name="summary",
    )(keys, values, col)

    def scan(value, way):
        other = lax.ppermute(value, "seq", swap_x)
        early_first = (x == 0) if way == 1 else (x == 1)
        early = jnp.where(early_first, value, other)
        late = jnp.where(early_first, other, value)
        total = join(early, late)
        carried = None
        step = 1
        while step < depth:
            got = shift(total, way * step)
            carried = got if carried is None else join(got, carried)
            step *= 2
            if step < depth:
                total = join(got, total)
        edge = docs[0] if way == 1 else docs[-1]

        def only(item):
            same = item[-1:, :1].astype(F32) == edge
            return jnp.where(same, item[:-PAD].astype(F32), 0.0)

        near = jnp.where(early_first, 0.0, only(other))
        result = near
        if carried is not None:
            result = result + only(carried)
        return result.astype(BF)

    state = scan(summary, 1)
    attn, normed = pl.pallas_call(
        attn_kernel,
        grid=(heads,),
        in_specs=[head_spec, head_spec, head_spec, state_spec, col_spec, row_spec, gain_spec],
        out_specs=[head_spec, head_spec],
        out_shape=[jax.ShapeDtypeStruct((rows, feats), F32), wide],
        cost_estimate=cost(5 * rows * rows * feats, 12 * rows * feats),
        name="attn",
    )(queries, keys, values, state, col, row, gain)

    theirs_all = gather_tp(theirs)
    stacked = jnp.stack(
        [
            jnp.concatenate([lax.dynamic_slice(mine, (0, x * mrows), (rows, mrows)), far], axis=0)
            for mine, far in zip(whole, theirs_all)
        ]
    )

    parts = 2
    each = feats // parts
    results = []
    for c in range(parts):
        mine = normed[:, c * each : (c + 1) * each]
        pair = jnp.concatenate([mine, lax.ppermute(mine, "seq", swap_x)], axis=0)

        def partial(dest, pair=pair):
            picked = lax.dynamic_index_in_dim(
                stacked, jnp.clip(dest, 0, depth - 1) ^ j, axis=0, keepdims=False
            )
            return dot(picked, pair, 0, 0) * factor

        up = None
        down = None
        for t in range(depth - 1):
            up_dest = depth - 1 - t + z
            down_dest = z - depth + 1 + t
            if 2 * t < depth - 1:
                one = partial(jnp.where(z <= t, up_dest, down_dest))
                ups = downs = one
            else:
                ups = partial(up_dest)
                downs = partial(down_dest)
            if up is not None:
                ups = ups + up.astype(F32)
                downs = downs + down.astype(F32)
            up_pairs = [(i, i + xs) for i in range(n) if i // xs <= t and i + xs < n]
            down_pairs = [(i, i - xs) for i in range(n) if i // xs >= depth - 1 - t and i >= xs]
            up = lax.ppermute(ups.astype(BF), "seq", up_pairs)
            down = lax.ppermute(downs.astype(BF), "seq", down_pairs)
        total = partial(z)
        if up is not None:
            total = total + up.astype(F32) + down.astype(F32)
        results.append(total)
    weight_grad = jnp.concatenate(results, axis=1)

    stacked_whole = jnp.stack(whole)
    order = jnp.arange(tp, dtype=jnp.int32) ^ j
    group = 256 if feats % 256 == 0 else HEAD
    two = pl.BlockSpec((rows, group), lambda h, o: (0, h))
    grad_attn, back_sum = pl.pallas_call(
        upstream_kernel,
        grid_spec=pltpu.PrefetchScalarGridSpec(
            num_scalar_prefetch=1,
            grid=(feats // group,),
            in_specs=[
                pl.BlockSpec((tp, rows, width), lambda h, o: (0, 0, 0)),
                pl.BlockSpec((group, model), lambda h, o: (h, 0)),
                two,
                two,
                pl.BlockSpec((rows, 1), lambda h, o: (0, 0)),
                pl.BlockSpec((1, group), lambda h, o: (0, h)),
            ],
            out_specs=[two, pl.BlockSpec((feats + PAD, HEAD), lambda h, o: (0, 0))],
        ),
        out_shape=[wide, sum_shape],
        cost_estimate=cost(2 * rows * model * feats, 2 * model * feats),
        name="upstream",
    )(order, stacked_whole, out_weight, queries, attn, col, gain)

    dstate = scan(back_sum, -1)
    query_grad, key_grad, value_grad = pl.pallas_call(
        grads_kernel,
        grid=(heads,),
        in_specs=[head_spec] * 4 + [state_spec] * 2 + [col_spec, row_spec],
        out_specs=[head_spec] * 3,
        out_shape=[wide] * 3,
        cost_estimate=cost(12 * rows * rows * feats, 14 * rows * feats),
        name="grads",
    )(queries, keys, values, grad_attn, state, dstate, col, row)
    return (query_grad, key_grad, value_grad, weight_grad)


def solution(mesh):
    wide = P("seq", "tp")
    in_specs = (wide, wide, wide, wide, P("tp", None), P("tp"), P("seq"))
    return jax.shard_map(
        local, mesh=mesh, in_specs=in_specs, out_specs=(wide,) * 4, check_vma=False
    )
```

```python
import functools
import math

import jax
import jax.numpy as jnp
from jax import lax
from jax.experimental import pallas as pl
from jax.experimental.pallas import tpu as pltpu
from jax.sharding import PartitionSpec as P

HEAD = 128
EPS = 1e-06
PAD = 16
BF = jnp.bfloat16
F32 = jnp.float32


def feature(x):
    return jnp.where(x > 0, x + 1.0, jnp.exp(jnp.minimum(x, 0.0)))


def slope(x):
    return jnp.where(x > 0, 1.0, jnp.exp(jnp.minimum(x, 0.0)))


def dot(a, b, ca, cb):
    return lax.dot_general(a, b, (((ca,), (cb,)), ((), ())), preferred_element_type=F32)


def causal_mask(col, row):
    rows = col.shape[0]
    at = lax.broadcasted_iota(jnp.int32, (rows, rows), 0)
    to = lax.broadcasted_iota(jnp.int32, (rows, rows), 1)
    return (at >= to) & (col == row)


MESH = pl.DeviceIdType.MESH


def layer_kernel(
    dims, q_ref, k_ref, v_ref, go_hbm, w_hbm, gain_ref, col_ref, row_ref,
    oq_ref, ok_ref, ov_ref, ow_ref,
    whole, theirs, w_ref, attn_ref, pair, grad_ref, state, own, oth, ein, eout,
    acc, sent, got, lsem, tsem, xsem, psem, osem, esem, rsem,
):
    n, tp, depth, mrows, width, parts, factor = dims
    rows, feats = q_ref.shape
    heads = feats // HEAD
    hc = 2
    chunks = heads // hc
    body = hc * HEAD
    each = feats // parts
    me = lax.axis_index("seq")
    j = lax.axis_index("tp")
    x = me % 2
    z = me // 2
    mate = me + 1 - 2 * x
    bits = tp.bit_length() - 1
    last = depth - 1
    mine_at = pl.ds(pl.multiple_of(x * mrows, mrows), mrows)
    mate_at = pl.ds(pl.multiple_of((1 - x) * mrows, mrows), mrows)

    def rc(src, dst, sems, at, dev):
        return pltpu.make_async_remote_copy(
            src_ref=src, dst_ref=dst, send_sem=sems.at[0, at], recv_sem=sems.at[1, at],
            device_id=dev, device_id_type=MESH,
        )

    def peer(b):
        bit = 1 << b
        return {"tp": j + bit * (1 - 2 * ((j // bit) % 2))}

    load_go = pltpu.make_async_copy(go_hbm, whole.at[0], lsem.at[0])
    load_w = pltpu.make_async_copy(w_hbm, w_ref, lsem.at[1])
    load_go.start()
    load_w.start()

    barrier = pltpu.get_barrier_semaphore()
    fixed = [{"seq": mate}] + [peer(b) for b in range(bits)]
    for dev in fixed:
        pl.semaphore_signal(barrier, inc=1, device_id=dev, device_id_type=MESH)

    @pl.when(z > 0)
    def _():
        pl.semaphore_signal(barrier, inc=1, device_id={"seq": me - 2}, device_id_type=MESH)

    @pl.when(z < last)
    def _():
        pl.semaphore_signal(barrier, inc=1, device_id={"seq": me + 2}, device_id_type=MESH)

    sides = (z + depth - 1) // depth + (last - z + depth - 1) // depth
    pl.semaphore_wait(barrier, len(fixed) + sides)

    def piece(buf, off, k, b):
        return rc(buf.at[k], buf.at[k | (1 << b)], tsem, off + (k | (1 << b)), peer(b))

    def forward(buf, off, k):
        low = bits if k == 0 else (k & -k).bit_length() - 1
        for b in reversed(range(low)):
            piece(buf, off, k, b).start()

    def arrived(buf, off, k):
        b = (k & -k).bit_length() - 1
        piece(buf, off, k ^ (1 << b), b).wait_recv()

    load_go.wait()
    swap = rc(whole.at[0, :, mate_at], theirs.at[0], tsem, 0, {"seq": mate})
    col = col_ref[...]
    first = col[0:1, :]
    final = col[rows - 1 : rows, :]

    forward(whole, 0, 0)

    def relay(buf, off, upto):
        for k in range(1, tp):
            if ((k & -k) > 1) == upto:
                arrived(buf, off, k)
                forward(buf, off, k)

    def swap_copy(w, c):
        return rc(own.at[w, c], oth.at[w, c], osem, w * chunks + c, {"seq": mate})

    def carry_copy(w, c):
        return rc(eout.at[w, c], ein.at[w, c], esem, w * chunks + c, {"seq": lax.rem(me + 2 - 4 * w + n, n)})

    def put(w, c, left, right_at, edge):
        for i in range(hc):
            own[w, c, i * HEAD : (i + 1) * HEAD, :] = dot(left[i], right_at[i], 0, 0).astype(BF)
        own[w, c, body:, :] = jnp.broadcast_to(edge, (PAD, HEAD)).astype(BF)
        swap_copy(w, c).start()

    def carry_on(w, c):
        begins = (z == 0) if w == 0 else (z == last)
        ends = (z == last) if w == 0 else (z == 0)
        edge = first if w == 0 else final
        swap_copy(w, c).wait_recv()

        @pl.when(begins)
        def _():
            ein[w, c] = jnp.zeros(ein.shape[2:], BF)

        @pl.when(jnp.logical_not(begins))
        def _():
            carry_copy(w, c).wait_recv()

        def tag(ref):
            return ref[w, c, body : body + 1, :].astype(F32)

        a = own[w, c, :body, :].astype(F32)
        b = oth[w, c, :body, :].astype(F32)
        e = ein[w, c, :body, :].astype(F32)
        ta, tb, te = tag(own), tag(oth), tag(ein)
        front = x == w

        @pl.when(jnp.logical_not(ends))
        def _():
            late_tag = jnp.where(front, tb, ta)
            same = jnp.where(ta == tb, 1.0, 0.0)
            keep_a = jnp.where(front, same, 1.0)
            keep_b = jnp.where(front, 1.0, same)
            keep_e = jnp.where(te == late_tag, 1.0, 0.0)
            eout[w, c, :body, :] = (a * keep_a + b * keep_b + e * keep_e).astype(BF)
            eout[w, c, body:, :] = jnp.broadcast_to(late_tag, (PAD, HEAD)).astype(BF)
            carry_copy(w, c).start()

        near = jnp.where(front, 0.0, jnp.where(tb == edge, 1.0, 0.0))
        far = jnp.where(te == edge, 1.0, 0.0)
        state[w, c * body : (c + 1) * body, :] = (b * near + e * far).astype(BF)

    for c in range(chunks):
        ats = [slice((c * hc + i) * HEAD, (c * hc + i + 1) * HEAD) for i in range(hc)]
        picked = [
            jnp.where(col == final, feature(k_ref[:, at].astype(F32)), 0.0).astype(BF) for at in ats
        ]
        put(0, c, picked, [v_ref[:, at] for at in ats], final)
    swap.start()
    for c in range(chunks):
        carry_on(0, c)
    swap.wait_recv()
    forward(theirs, tp, 0)

    def pair_copy(c):
        return rc(pair.at[c, 0], pair.at[c, 1], psem, c, {"seq": mate})

    per = each // HEAD
    for c in range(parts):

        @pl.loop(0, per)
        def _(i):
            at = pl.ds(pl.multiple_of(c * each + i * HEAD, HEAD), HEAD)
            to = pl.ds(pl.multiple_of(i * HEAD, HEAD), HEAD)
            fq = feature(q_ref[:, at].astype(F32)).astype(BF)
            fk = feature(k_ref[:, at].astype(F32)).astype(BF)
            mask = causal_mask(col, row_ref[...])
            weight = jnp.where(mask, dot(fq, fk, 1, 1), 0.0).astype(BF)
            attn = dot(weight, v_ref[:, at], 1, 0)
            attn = attn + jnp.where(col == first, dot(fq, state[0, at, :], 1, 0), 0.0)
            inv = lax.rsqrt(jnp.mean(attn * attn, axis=-1, keepdims=True) + EPS)
            attn_ref[:, at] = attn
            pair[c, 0, :, to] = (attn * inv * gain_ref[:, at]).astype(BF)

        pair_copy(c).start()
    relay(whole, 0, True)
    relay(theirs, tp, True)
    relay(whole, 0, False)
    relay(theirs, tp, False)

    def partial(c, dest):
        k = jnp.int32(0)
        for b in range(bits):
            k = k + (1 << b) * ((dest // (1 << b) + j // (1 << b)) % 2)
        value = dot(whole[k, :, mine_at], pair[c, 0], 0, 0) + dot(theirs[k], pair[c, 1], 0, 0)
        return value * factor

    def chain(w, c, t):
        at = (w * parts + c) * last + t
        return rc(
            sent.at[w, c, t], got.at[w, c, t], rsem, at, {"seq": lax.rem(me + 2 - 4 * w + n, n)}
        )

    def on_way(w, t):
        return (z <= t) if w == 0 else (z >= last - t)

    def send_step(w, c, t):
        @pl.when(on_way(w, t))
        def _():
            dest = last - t + z if w == 0 else z - last + t
            acc[...] = partial(c, dest)
            if t > 0:

                @pl.when((z > 0) if w == 0 else (z < last))
                def _():
                    chain(w, c, t - 1).wait_recv()
                    acc[...] += got[w, c, t - 1].astype(F32)

            sent[w, c, t] = acc[...].astype(BF)
            chain(w, c, t).start()

    for c in range(parts):
        pair_copy(c).wait_recv()
        for w in range(2):
            send_step(w, c, 0)

    load_w.wait()
    for c in range(chunks):
        at = slice(c * body, (c + 1) * body)
        total = None
        for k in range(tp):
            owner = jnp.int32(0)
            for b in range(bits):
                owner = owner + (1 << b) * (((k >> b) + j // (1 << b)) % 2)
            start = pl.multiple_of(owner * width, width)
            term = dot(whole[k], w_ref[at, pl.ds(start, width)], 1, 1)
            total = term if total is None else total + term
        left, right = [], []
        for i in range(hc):
            cut = slice(c * body + i * HEAD, c * body + (i + 1) * HEAD)
            attn = attn_ref[:, cut]
            inv = lax.rsqrt(jnp.mean(attn * attn, axis=-1, keepdims=True) + EPS)
            scaled = total[:, i * HEAD : (i + 1) * HEAD] * gain_ref[:, cut]
            mean = jnp.mean(attn * scaled, axis=-1, keepdims=True)
            grad = (scaled * inv - attn * (inv * inv * inv) * mean).astype(BF)
            grad_ref[:, cut] = grad
            left.append(jnp.where(col == first, feature(q_ref[:, cut].astype(F32)), 0.0).astype(BF))
            right.append(grad)
        put(1, c, left, right, first)

    def grads(begin, end):
        @pl.loop(begin, end)
        def _(h):
            at = pl.ds(pl.multiple_of(h * HEAD, HEAD), HEAD)
            mask = causal_mask(col, row_ref[...])
            q = q_ref[:, at].astype(F32)
            k = k_ref[:, at].astype(F32)
            v = v_ref[:, at]
            g = grad_ref[:, at]
            fq = feature(q).astype(BF)
            fk = feature(k).astype(BF)
            weight = jnp.where(mask, dot(fq, fk, 1, 1), 0.0).astype(BF)
            gw = jnp.where(mask, dot(g, v, 1, 1), 0.0).astype(BF)
            early = col == first
            late = col == final
            s = state[0, at, :]
            d = state[1, at, :]
            vp = dot(weight, g, 0, 0) + jnp.where(late, dot(fk, d, 1, 0), 0.0)
            ov_ref[:, at] = vp.astype(BF)
            kp = dot(gw, fq, 0, 0) + jnp.where(late, dot(v, d, 1, 1), 0.0)
            ok_ref[:, at] = (kp * slope(k)).astype(BF)
            qp = dot(gw, fk, 1, 0) + jnp.where(early, dot(g, s, 1, 1), 0.0)
            oq_ref[:, at] = (qp * slope(q)).astype(BF)

    def steps(t):
        for c in range(parts):
            for w in range(2):
                send_step(w, c, t)

    for t in range(1, min(2, last)):
        steps(t)
    for c in range(chunks):
        carry_on(1, c)
    grads(0, heads // 2)
    for t in range(2, last):
        steps(t)
    grads(heads // 2, heads)
    for c in range(parts):
        ow_ref[:, c * each : (c + 1) * each] = partial(c, z)
    for c in range(parts):
        for w in range(2):

            @pl.when((z > 0) if w == 0 else (z < last))
            def _():
                chain(w, c, last - 1).wait_recv()
                ow_ref[:, c * each : (c + 1) * each] += got[w, c, last - 1].astype(F32)

    swap.wait_send()
    for buf, off in ((whole, 0), (theirs, tp)):
        for k in range(1, tp):
            b = (k & -k).bit_length() - 1
            piece(buf, off, k ^ (1 << b), b).wait_send()
    for c in range(parts):
        pair_copy(c).wait_send()
    for w in range(2):
        for c in range(chunks):
            swap_copy(w, c).wait_send()

            @pl.when((z < last) if w == 0 else (z > 0))
            def _():
                carry_copy(w, c).wait_send()

        for c in range(parts):
            for t in range(last):

                @pl.when(on_way(w, t))
                def _():
                    chain(w, c, t).wait_send()


def local(queries, keys, values, grad_out, out_weight, norm_gain, doc_ids):
    rows, feats = queries.shape
    n = lax.axis_size("seq")
    tp = lax.axis_size("tp")
    depth = n // 2
    model = out_weight.shape[1]
    width = model // tp
    mrows = model // n
    parts = 2
    each = feats // parts
    heads = feats // HEAD
    chunks = heads // 2
    last = depth - 1
    docs = doc_ids.astype(F32)
    dims = (n, tp, depth, mrows, width, parts, 1.0 / math.sqrt(rows * n))
    vmem = pl.BlockSpec(memory_space=pltpu.VMEM)
    anyspace = pl.BlockSpec(memory_space=pl.ANY)
    wide = jax.ShapeDtypeStruct((rows, feats), BF)
    summed = pltpu.VMEM((2, chunks, 2 * HEAD + PAD, HEAD), BF)
    sem = pltpu.SemaphoreType.DMA
    flops = 2 * rows * model * feats * 3
    return pl.pallas_call(
        functools.partial(layer_kernel, dims),
        in_specs=[vmem] * 3 + [anyspace] * 2 + [vmem] * 3,
        out_specs=[vmem] * 4,
        out_shape=[wide] * 3 + [jax.ShapeDtypeStruct((mrows, feats), F32)],
        scratch_shapes=[
            pltpu.VMEM((tp, rows, width), BF),
            pltpu.VMEM((tp, rows, mrows), BF),
            pltpu.VMEM((feats, model), BF),
            pltpu.VMEM((rows, feats), F32),
            pltpu.VMEM((parts, 2, rows, each), BF),
            pltpu.VMEM((rows, feats), BF),
            pltpu.VMEM((2, feats, HEAD), BF),
            summed, summed, summed, summed,
            pltpu.VMEM((mrows, each), F32),
            pltpu.VMEM((2, parts, last, mrows, each), BF),
            pltpu.VMEM((2, parts, last, mrows, each), BF),
            sem((2,)),
            sem((2, 2 * tp)),
            sem((2, 1)),
            sem((2, parts)),
            sem((2, 2 * chunks)),
            sem((2, 2 * chunks)),
            sem((2, 2 * parts * last)),
        ],
        compiler_params=pltpu.CompilerParams(
            collective_id=0, has_side_effects=True, vmem_limit_bytes=60 * 1024 * 1024
        ),
        cost_estimate=pl.CostEstimate(flops=flops, bytes_accessed=flops // 512, transcendentals=0),
        name="layer",
    )(queries, keys, values, grad_out, out_weight, norm_gain[None, :], docs[:, None], docs[None, :])


def solution(mesh):
    wide = P("seq", "tp")
    in_specs = (wide, wide, wide, wide, P("tp", None), P("tp"), P("seq"))
    return jax.shard_map(
        local, mesh=mesh, in_specs=in_specs, out_specs=(wide,) * 4, check_vma=False
    )
```

```python
import functools
import math

import jax
import jax.numpy as jnp
from jax import lax
from jax.experimental import pallas as pl
from jax.experimental.pallas import tpu as pltpu
from jax.sharding import PartitionSpec as P

HEAD = 128
EPS = 1e-06
PAD = 16
BF = jnp.bfloat16
F32 = jnp.float32


def feature(x):
    return jnp.where(x > 0, x + 1.0, jnp.exp(jnp.minimum(x, 0.0)))


def slope(x):
    return jnp.where(x > 0, 1.0, jnp.exp(jnp.minimum(x, 0.0)))


def dot(a, b, ca, cb):
    return lax.dot_general(a, b, (((ca,), (cb,)), ((), ())), preferred_element_type=F32)


def causal_mask(col, row):
    rows = col.shape[0]
    at = lax.broadcasted_iota(jnp.int32, (rows, rows), 0)
    to = lax.broadcasted_iota(jnp.int32, (rows, rows), 1)
    return (at >= to) & (col == row)


MESH = pl.DeviceIdType.MESH


def layer_kernel(
    dims, q_ref, k_ref, v_ref, go_hbm, w_hbm, gain_ref, col_ref, row_ref,
    oq_ref, ok_ref, ov_ref, ow_ref,
    whole, theirs, w_ref, attn_ref, pair, grad_ref, state, own, oth, ein, eout,
    acc, sent, got, lsem, tsem, xsem, psem, osem, esem, rsem,
):
    n, tp, depth, mrows, width, parts, factor = dims
    rows, feats = q_ref.shape
    heads = feats // HEAD
    hc = 2
    chunks = heads // hc
    body = hc * HEAD
    each = feats // parts
    me = lax.axis_index("seq")
    j = lax.axis_index("tp")
    x = me % 2
    z = me // 2
    mate = me + 1 - 2 * x
    bits = tp.bit_length() - 1
    last = depth - 1
    mine_at = pl.ds(pl.multiple_of(x * mrows, mrows), mrows)
    mate_at = pl.ds(pl.multiple_of((1 - x) * mrows, mrows), mrows)

    def rc(src, dst, sems, at, dev):
        return pltpu.make_async_remote_copy(
            src_ref=src, dst_ref=dst, send_sem=sems.at[0, at], recv_sem=sems.at[1, at],
            device_id=dev, device_id_type=MESH,
        )

    def peer(b):
        bit = 1 << b
        return {"tp": j + bit * (1 - 2 * ((j // bit) % 2))}

    load_go = pltpu.make_async_copy(go_hbm, whole.at[0], lsem.at[0])
    load_w = pltpu.make_async_copy(w_hbm, w_ref, lsem.at[1])
    load_go.start()
    load_w.start()

    barrier = pltpu.get_barrier_semaphore()
    fixed = [{"seq": mate}] + [peer(b) for b in range(bits)]
    for dev in fixed:
        pl.semaphore_signal(barrier, inc=1, device_id=dev, device_id_type=MESH)

    @pl.when(z > 0)
    def _():
        pl.semaphore_signal(barrier, inc=1, device_id={"seq": me - 2}, device_id_type=MESH)

    @pl.when(z < last)
    def _():
        pl.semaphore_signal(barrier, inc=1, device_id={"seq": me + 2}, device_id_type=MESH)

    sides = (z + depth - 1) // depth + (last - z + depth - 1) // depth
    pl.semaphore_wait(barrier, len(fixed) + sides)

    def piece(buf, off, k, b):
        return rc(buf.at[k], buf.at[k | (1 << b)], tsem, off + (k | (1 << b)), peer(b))

    def forward(buf, off, k):
        low = bits if k == 0 else (k & -k).bit_length() - 1
        for b in reversed(range(low)):
            piece(buf, off, k, b).start()

    def arrived(buf, off, k):
        b = (k & -k).bit_length() - 1
        piece(buf, off, k ^ (1 << b), b).wait_recv()

    load_go.wait()
    swap = rc(whole.at[0, :, mate_at], theirs.at[0], tsem, 0, {"seq": mate})
    col = col_ref[...]
    first = col[0:1, :]
    final = col[rows - 1 : rows, :]

    forward(whole, 0, 0)

    def relay(buf, off, upto):
        for k in range(1, tp):
            if ((k & -k) > 1) == upto:
                arrived(buf, off, k)
                forward(buf, off, k)

    def swap_copy(w, c):
        return rc(own.at[w, c], oth.at[w, c], osem, w * chunks + c, {"seq": mate})

    def carry_copy(w, c):
        return rc(eout.at[w, c], ein.at[w, c], esem, w * chunks + c, {"seq": lax.rem(me + 2 - 4 * w + n, n)})

    def put(w, c, left, right_at, edge):
        for i in range(hc):
            own[w, c, i * HEAD : (i + 1) * HEAD, :] = dot(left[i], right_at[i], 0, 0).astype(BF)
        own[w, c, body:, :] = jnp.broadcast_to(edge, (PAD, HEAD)).astype(BF)
        swap_copy(w, c).start()

    def carry_on(w, c):
        begins = (z == 0) if w == 0 else (z == last)
        ends = (z == last) if w == 0 else (z == 0)
        edge = first if w == 0 else final
        swap_copy(w, c).wait_recv()

        @pl.when(begins)
        def _():
            ein[w, c] = jnp.zeros(ein.shape[2:], BF)

        @pl.when(jnp.logical_not(begins))
        def _():
            carry_copy(w, c).wait_recv()

        def tag(ref):
            return ref[w, c, body : body + 1, :].astype(F32)

        a = own[w, c, :body, :].astype(F32)
        b = oth[w, c, :body, :].astype(F32)
        e = ein[w, c, :body, :].astype(F32)
        ta, tb, te = tag(own), tag(oth), tag(ein)
        front = x == w

        @pl.when(jnp.logical_not(ends))
        def _():
            late_tag = jnp.where(front, tb, ta)
            same = jnp.where(ta == tb, 1.0, 0.0)
            keep_a = jnp.where(front, same, 1.0)
            keep_b = jnp.where(front, 1.0, same)
            keep_e = jnp.where(te == late_tag, 1.0, 0.0)
            eout[w, c, :body, :] = (a * keep_a + b * keep_b + e * keep_e).astype(BF)
            eout[w, c, body:, :] = jnp.broadcast_to(late_tag, (PAD, HEAD)).astype(BF)
            carry_copy(w, c).start()

        near = jnp.where(front, 0.0, jnp.where(tb == edge, 1.0, 0.0))
        far = jnp.where(te == edge, 1.0, 0.0)
        state[w, c * body : (c + 1) * body, :] = (b * near + e * far).astype(BF)

    for c in range(chunks):
        ats = [slice((c * hc + i) * HEAD, (c * hc + i + 1) * HEAD) for i in range(hc)]
        picked = [
            jnp.where(col == final, feature(k_ref[:, at].astype(F32)), 0.0).astype(BF) for at in ats
        ]
        put(0, c, picked, [v_ref[:, at] for at in ats], final)
    swap.start()
    for c in range(chunks):
        carry_on(0, c)
    swap.wait_recv()
    forward(theirs, tp, 0)

    def pair_copy(c):
        return rc(pair.at[c, 0], pair.at[c, 1], psem, c, {"seq": mate})

    per = each // HEAD
    for c in range(parts):

        @pl.loop(0, per)
        def _(i):
            at = pl.ds(pl.multiple_of(c * each + i * HEAD, HEAD), HEAD)
            to = pl.ds(pl.multiple_of(i * HEAD, HEAD), HEAD)
            fq = feature(q_ref[:, at].astype(F32)).astype(BF)
            fk = feature(k_ref[:, at].astype(F32)).astype(BF)
            mask = causal_mask(col, row_ref[...])
            weight = jnp.where(mask, dot(fq, fk, 1, 1), 0.0).astype(BF)
            attn = dot(weight, v_ref[:, at], 1, 0)
            attn = attn + jnp.where(col == first, dot(fq, state[0, at, :], 1, 0), 0.0)
            inv = lax.rsqrt(jnp.mean(attn * attn, axis=-1, keepdims=True) + EPS)
            attn_ref[:, at] = attn
            pair[c, 0, :, to] = (attn * inv * gain_ref[:, at]).astype(BF)

        pair_copy(c).start()
    relay(whole, 0, True)
    relay(theirs, tp, True)
    relay(whole, 0, False)
    relay(theirs, tp, False)

    def partial(c, dest):
        k = jnp.int32(0)
        for b in range(bits):
            k = k + (1 << b) * ((dest // (1 << b) + j // (1 << b)) % 2)
        value = dot(whole[k, :, mine_at], pair[c, 0], 0, 0) + dot(theirs[k], pair[c, 1], 0, 0)
        return value * factor

    def chain(w, c, t):
        at = (w * parts + c) * last + t
        return rc(
            sent.at[w, c, t], got.at[w, c, t], rsem, at, {"seq": lax.rem(me + 2 - 4 * w + n, n)}
        )

    def on_way(w, t):
        return (z <= t) if w == 0 else (z >= last - t)

    def send_step(w, c, t, when):
        @pl.when(when)
        def _():
            dest = last - t + z if w == 0 else z - last + t
            acc[...] = partial(c, dest)
            if t > 0:

                @pl.when((z > 0) if w == 0 else (z < last))
                def _():
                    chain(w, c, t - 1).wait_recv()
                    acc[...] += got[w, c, t - 1].astype(F32)

            sent[w, c, t] = acc[...].astype(BF)
            chain(w, c, t).start()

    for c in range(parts):
        pair_copy(c).wait_recv()
        for w in range(2):
            send_step(w, c, 0, on_way(w, 0))

    load_w.wait()
    for c in range(chunks):
        at = slice(c * body, (c + 1) * body)
        total = None
        for k in range(tp):
            owner = jnp.int32(0)
            for b in range(bits):
                owner = owner + (1 << b) * (((k >> b) + j // (1 << b)) % 2)
            start = pl.multiple_of(owner * width, width)
            term = dot(whole[k], w_ref[at, pl.ds(start, width)], 1, 1)
            total = term if total is None else total + term
        left, right = [], []
        for i in range(hc):
            cut = slice(c * body + i * HEAD, c * body + (i + 1) * HEAD)
            attn = attn_ref[:, cut]
            inv = lax.rsqrt(jnp.mean(attn * attn, axis=-1, keepdims=True) + EPS)
            scaled = total[:, i * HEAD : (i + 1) * HEAD] * gain_ref[:, cut]
            mean = jnp.mean(attn * scaled, axis=-1, keepdims=True)
            grad = (scaled * inv - attn * (inv * inv * inv) * mean).astype(BF)
            grad_ref[:, cut] = grad
            left.append(jnp.where(col == first, feature(q_ref[:, cut].astype(F32)), 0.0).astype(BF))
            right.append(grad)
        put(1, c, left, right, first)

    def grads(begin, end):
        @pl.loop(begin, end)
        def _(h):
            at = pl.ds(pl.multiple_of(h * HEAD, HEAD), HEAD)
            mask = causal_mask(col, row_ref[...])
            q = q_ref[:, at].astype(F32)
            k = k_ref[:, at].astype(F32)
            v = v_ref[:, at]
            g = grad_ref[:, at]
            fq = feature(q).astype(BF)
            fk = feature(k).astype(BF)
            weight = jnp.where(mask, dot(fq, fk, 1, 1), 0.0).astype(BF)
            gw = jnp.where(mask, dot(g, v, 1, 1), 0.0).astype(BF)
            early = col == first
            late = col == final
            s = state[0, at, :]
            d = state[1, at, :]
            vp = dot(weight, g, 0, 0) + jnp.where(late, dot(fk, d, 1, 0), 0.0)
            ov_ref[:, at] = vp.astype(BF)
            kp = dot(gw, fq, 0, 0) + jnp.where(late, dot(v, d, 1, 1), 0.0)
            ok_ref[:, at] = (kp * slope(k)).astype(BF)
            qp = dot(gw, fk, 1, 0) + jnp.where(early, dot(g, s, 1, 1), 0.0)
            oq_ref[:, at] = (qp * slope(q)).astype(BF)

    def steps(t):
        for c in range(parts):
            for w in range(2):
                send_step(w, c, t, on_way(w, t) & (z > 0) if w == 0 else on_way(w, t))

    for t in range(1, last):
        for c in range(parts):
            send_step(0, c, t, z == 0)
    for c in range(chunks):
        carry_on(1, c)
    for t in range(1, min(2, last)):
        steps(t)
    grads(0, heads // 2)
    for t in range(2, last):
        steps(t)
    grads(heads // 2, heads)
    for c in range(parts):
        ow_ref[:, c * each : (c + 1) * each] = partial(c, z)
    for c in range(parts):
        for w in range(2):

            @pl.when((z > 0) if w == 0 else (z < last))
            def _():
                chain(w, c, last - 1).wait_recv()
                ow_ref[:, c * each : (c + 1) * each] += got[w, c, last - 1].astype(F32)

    swap.wait_send()
    for buf, off in ((whole, 0), (theirs, tp)):
        for k in range(1, tp):
            b = (k & -k).bit_length() - 1
            piece(buf, off, k ^ (1 << b), b).wait_send()
    for c in range(parts):
        pair_copy(c).wait_send()
    for w in range(2):
        for c in range(chunks):
            swap_copy(w, c).wait_send()

            @pl.when((z < last) if w == 0 else (z > 0))
            def _():
                carry_copy(w, c).wait_send()

        for c in range(parts):
            for t in range(last):

                @pl.when(on_way(w, t))
                def _():
                    chain(w, c, t).wait_send()


def local(queries, keys, values, grad_out, out_weight, norm_gain, doc_ids):
    rows, feats = queries.shape
    n = lax.axis_size("seq")
    tp = lax.axis_size("tp")
    depth = n // 2
    model = out_weight.shape[1]
    width = model // tp
    mrows = model // n
    parts = 2
    each = feats // parts
    heads = feats // HEAD
    chunks = heads // 2
    last = depth - 1
    docs = doc_ids.astype(F32)
    dims = (n, tp, depth, mrows, width, parts, 1.0 / math.sqrt(rows * n))
    vmem = pl.BlockSpec(memory_space=pltpu.VMEM)
    anyspace = pl.BlockSpec(memory_space=pl.ANY)
    wide = jax.ShapeDtypeStruct((rows, feats), BF)
    summed = pltpu.VMEM((2, chunks, 2 * HEAD + PAD, HEAD), BF)
    sem = pltpu.SemaphoreType.DMA
    flops = 2 * rows * model * feats * 3
    return pl.pallas_call(
        functools.partial(layer_kernel, dims),
        in_specs=[vmem] * 3 + [anyspace] * 2 + [vmem] * 3,
        out_specs=[vmem] * 4,
        out_shape=[wide] * 3 + [jax.ShapeDtypeStruct((mrows, feats), F32)],
        scratch_shapes=[
            pltpu.VMEM((tp, rows, width), BF),
            pltpu.VMEM((tp, rows, mrows), BF),
            pltpu.VMEM((feats, model), BF),
            pltpu.VMEM((rows, feats), F32),
            pltpu.VMEM((parts, 2, rows, each), BF),
            pltpu.VMEM((rows, feats), BF),
            pltpu.VMEM((2, feats, HEAD), BF),
            summed, summed, summed, summed,
            pltpu.VMEM((mrows, each), F32),
            pltpu.VMEM((2, parts, last, mrows, each), BF),
            pltpu.VMEM((2, parts, last, mrows, each), BF),
            sem((2,)),
            sem((2, 2 * tp)),
            sem((2, 1)),
            sem((2, parts)),
            sem((2, 2 * chunks)),
            sem((2, 2 * chunks)),
            sem((2, 2 * parts * last)),
        ],
        compiler_params=pltpu.CompilerParams(
            collective_id=0, has_side_effects=True, vmem_limit_bytes=60 * 1024 * 1024
        ),
        cost_estimate=pl.CostEstimate(flops=flops, bytes_accessed=flops // 512, transcendentals=0),
        name="layer",
    )(queries, keys, values, grad_out, out_weight, norm_gain[None, :], docs[:, None], docs[None, :])


def solution(mesh):
    wide = P("seq", "tp")
    in_specs = (wide, wide, wide, wide, P("tp", None), P("tp"), P("seq"))
    return jax.shard_map(
        local, mesh=mesh, in_specs=in_specs, out_specs=(wide,) * 4, check_vma=False
    )
```
